512 devices in a mesh: section: 8 (over x, core), tm: 16 (over z_hi, y), dp: 4 (over z_lo).
Axes of the slice: x: 4, y: 4, z: 16 (z_hi: 4, z_lo: 4; z = z_hi * 4 + z_lo), core: 2. Of those that a mesh axis runs over, the one named last changes fastest.
Arguments:
- frames: bfloat16 [32, 8192, 512], P(('section', 'dp'), 'tm'), may hold values from -6 to 6
- lengths: int32 [32], P(('section', 'dp')), may hold values from 40960 to 163840, as said below
- fourth_conv: bfloat16 [3, 512, 512], P(None, ('section', 'dp')), may hold values from -0.15625 to 0.15625
- fifth_conv: bfloat16 [3, 512, 512], P(None, ('section', 'dp')), may hold values from -0.15625 to 0.15625
- sixth_conv: bfloat16 [2, 512, 512], P(None, ('section', 'dp')), may hold values from -0.1875 to 0.1875
- seventh_conv: bfloat16 [2, 512, 512], P(None, ('section', 'dp')), may hold values from -0.1875 to 0.1875
- norm_gain: float32 [512], replicated, may hold values from 0.5 to 1.5
- norm_bias: float32 [512], replicated, may hold values from -1.8 to 1.8
- project_weight: bfloat16 [512, 1920], P(None, 'tm'), may hold values from -0.25 to 0.25
- project_bias: bfloat16 [1, 1920], P(None, 'tm'), may hold values from -1.796875 to 1.796875
- position_weight: bfloat16 [16, 128, 14400], P('tm', ('section', 'dp')), may hold values from -0.046875 to 0.046875
- position_bias: float32 [1920], P('tm'), may hold values from -3 to 3
Outputs:
- encoded: bfloat16 [32, 1920, 512], P(('section', 'dp'), 'tm')
The draws below stay inside these ranges and needn't reach their ends.
Inputs may be any that keep to these rules, and one draw needn't show every extreme that they name: `lengths`: length of each utterance in samples; some utterance of every draw fills all 8192 input frames.
All inputs are finite; a program needn't handle non-finite values.
Results may differ from the reference program's by a relative error of at most 0.012.
Values may be sent and summed in bfloat16 or wider, within the bound.
A program may use at most 64 MiB of HBM per device.

```python
import jax
import jax.numpy as jnp
from jax import lax

CONV_DIM = 512
GROUP_WIDTH = 120
TAPS = 128
GROUPS = 16
HIDDEN_SIZE = 1920
FRAMES = 512
IN_FRAMES = 8192
UTTERANCES = 32


def draw_lengths(key, part):
    key_one, key_two = jax.random.split(jax.random.fold_in(key, 7))
    longest = IN_FRAMES * 20
    lengths_drawn = jax.random.randint(key_one, (UTTERANCES,), IN_FRAMES * 5, longest + 1, dtype=jnp.int32)
    chosen = jax.random.randint(key_two, (), 0, UTTERANCES, dtype=jnp.int32)
    return lengths_drawn.at[chosen].set(longest)


def block_scale(key, dims, cuts, low, largest):
    def one(dim, parts):
        heights = jax.random.uniform(jax.random.fold_in(jax.random.fold_in(key, 6), dim), (parts,), jnp.float32, low / len(cuts), largest / len(cuts))
        return jnp.repeat(jnp.exp(heights), dims[dim] // parts).reshape((-1,) + (1,) * (len(dims) - dim - 1))

    level = one(*cuts[0])
    for cut in cuts[1:]:
        level = level * one(*cut)
    return level


def noise(stream_key, shape, scale, reach, cuts=(), kind=jnp.bfloat16):
    gain = block_scale(stream_key, shape, cuts, -0.22, 0.18) if cuts else 1.0
    drawn = jax.random.normal(stream_key, shape, jnp.float32) * scale * gain
    return jnp.minimum(jnp.maximum(drawn, -reach), reach).astype(kind)


def setup_inputs(seed: int = 0) -> dict:
    seeds = jax.random.split(jax.random.key(seed), 13)
    frames = noise(seeds[0], (UTTERANCES, IN_FRAMES, CONV_DIM), 1.0, 6.0, ((0, 32), (1, 16)))
    lengths = draw_lengths(jax.random.fold_in(seeds[12], 71), 0)
    fourth_conv = noise(seeds[2], (3, CONV_DIM, CONV_DIM), (3 * CONV_DIM) ** -0.5, 0.15625, ((1, 32),))
    fifth_conv = noise(seeds[3], (3, CONV_DIM, CONV_DIM), (3 * CONV_DIM) ** -0.5, 0.15625, ((1, 32),))
    sixth_conv = noise(seeds[4], (2, CONV_DIM, CONV_DIM), (2 * CONV_DIM) ** -0.5, 0.1875, ((1, 32),))
    seventh_conv = noise(seeds[5], (2, CONV_DIM, CONV_DIM), (2 * CONV_DIM) ** -0.5, 0.1875, ((1, 32),))
    norm_gain = jnp.clip(1.0 + 0.1 * jax.random.normal(seeds[6], (CONV_DIM,), jnp.float32), 0.5, 1.5)
    norm_bias = noise(seeds[7], (CONV_DIM,), 0.3, 1.8, (), jnp.float32)
    project_weight = noise(seeds[8], (CONV_DIM, HIDDEN_SIZE), CONV_DIM ** -0.5, 0.25, ((1, 16),))
    project_bias = noise(seeds[9], (1, HIDDEN_SIZE), 0.3, 1.796875, ((1, 16),))
    position_weight = noise(seeds[10], (GROUPS, TAPS, GROUP_WIDTH * GROUP_WIDTH), (TAPS * GROUP_WIDTH) ** -0.5, 0.046875, ((0, 16), (1, 32)))
    position_bias = noise(seeds[11], (HIDDEN_SIZE,), 0.5, 3.0, ((0, 16),), jnp.float32)
    return {"frames": frames, "lengths": lengths, "fourth_conv": fourth_conv, "fifth_conv": fifth_conv, "sixth_conv": sixth_conv, "seventh_conv": seventh_conv, "norm_gain": norm_gain, "norm_bias": norm_bias, "project_weight": project_weight, "project_bias": project_bias, "position_weight": position_weight, "position_bias": position_bias}


eps_norm = 1e-05

def layer_norm(values):
    average = lax.optimization_barrier(jnp.mean(values, axis=-1, keepdims=True))
    centred = values - average
    spread = lax.optimization_barrier(jnp.mean(centred * centred, axis=-1, keepdims=True))
    return centred * lax.rsqrt(spread + eps_norm)

def strided_conv(inputs, weight):
    row_count = inputs.shape[0]
    channels = inputs.shape[1]
    padded = jnp.concatenate([inputs, jnp.zeros((2, channels), inputs.dtype)], axis=0)
    paired = padded.reshape(row_count // 2 + 1, 2, channels)
    even_rows = paired[:, 0]
    odd_rows = paired[:, 1]
    out_rows = row_count // 2
    summed = jnp.dot(even_rows[:out_rows], weight[0], preferred_element_type=jnp.float32)
    summed = summed + jnp.dot(odd_rows[:out_rows], weight[1], preferred_element_type=jnp.float32)
    if weight.shape[0] == 3:
        summed = summed + jnp.dot(even_rows[1:out_rows + 1], weight[2], preferred_element_type=jnp.float32)
    return jax.nn.gelu(layer_norm(summed), approximate=False).astype(jnp.bfloat16)

def reference(frames, lengths, fourth_conv, fifth_conv, sixth_conv, seventh_conv, norm_gain, norm_bias, project_weight, project_bias, position_weight, position_bias):
    kernel = position_weight.astype(jnp.float32).reshape(GROUPS, TAPS, GROUP_WIDTH, GROUP_WIDTH)
    kernel = kernel.transpose(0, 2, 3, 1).reshape(HIDDEN_SIZE, GROUP_WIDTH, TAPS)

    def one_utterance(members):
        inputs, length = members
        sample_index = jnp.arange(IN_FRAMES, dtype=jnp.int32)
        current = jnp.where((sample_index * 20 < length)[:, None], inputs, jnp.zeros_like(inputs))
        for weight in (fourth_conv, fifth_conv, sixth_conv, seventh_conv):
            current = strided_conv(current, weight)
        normed = (layer_norm(current.astype(jnp.float32)) * norm_gain + norm_bias).astype(jnp.bfloat16)
        hidden = (jnp.dot(normed, project_weight, preferred_element_type=jnp.float32) + project_bias.astype(jnp.float32)).astype(jnp.bfloat16)
        frame_index = jnp.arange(FRAMES, dtype=jnp.int32)
        hidden = jnp.where((frame_index * 320 < length)[:, None], hidden, jnp.zeros_like(hidden))
        channels_first = hidden.astype(jnp.float32).T
        conv = lax.conv_general_dilated(channels_first[None], kernel, (1,), [(TAPS // 2, TAPS // 2 - 1)], dimension_numbers=('NCH', 'OIH', 'NCH'), feature_group_count=GROUPS, precision=lax.Precision.HIGHEST)[0]
        position = jax.nn.gelu(conv + position_bias[:, None], approximate=False)
        return (channels_first + position).astype(jnp.bfloat16)
    return lax.map(one_utterance, (frames, lengths))
```

```python
import functools

import jax
import jax.numpy as jnp
from jax import lax
from jax.experimental import pallas as pl
from jax.experimental.pallas import tpu as pltpu
from jax.sharding import PartitionSpec as P

MESH = pl.DeviceIdType.MESH
CH = 512
GW = 120
EPS = 1e-05
HALO = 16
ROWS4 = 272
GROUPS_OF_TAPS = ((0, 1), (2, 3), (4, 5), (6, 7), (8, 9))
N_TAPS = 10


def norm(values):
    average = jnp.mean(values, axis=-1, keepdims=True)
    centred = values - average
    spread = jnp.mean(centred * centred, axis=-1, keepdims=True)
    return centred * lax.rsqrt(spread + EPS)


def gelu(values):
    return 0.5 * values * (1.0 + lax.erf(values * 0.7071067811865476))


def kernel(
    len_ref, frames_ref, w4_ref, w5_ref, w6_ref, w7_ref, gain_ref, nbias_ref,
    pw_ref, pb_ref, pos_ref, posb_ref, out_ref,
    wbuf, pbuf, halo, x4, x5, x6, x7, nbuf, hf, x16,
    local_sem, w_send, w_recv, p_send, p_recv, a_send, a_recv, h_send, h_recv,
):
    section = lax.axis_index("section")
    tm = lax.axis_index("tm")
    zl = lax.axis_index("dp")
    xi = section // 2
    core = lax.rem(section, 2)
    zh = tm // 4
    y = lax.rem(tm, 4)
    direction = 1 - 2 * core

    def at_x(by):
        return (lax.rem(xi + by + 4, 4) * 2 + core, tm, zl)

    def at_z(by):
        z = lax.rem(zh * 4 + zl + by + 16, 16)
        return (section, (z // 4) * 4 + y, lax.rem(z, 4))

    def at_line(by):
        return (section, tm, lax.rem(zl + by, 4))

    def at_zh(by):
        return (section, lax.rem(zh + by, 4) * 4 + y, zl)

    def at_y(by):
        return (section, zh * 4 + lax.rem(y + by, 4), zl)

    partner = (xi * 2 + 1 - core, tm, zl)
    before = (section, lax.rem(tm + 15, 16), zl)
    after = (section, lax.rem(tm + 1, 16), zl)

    greeted = [at_x(1), at_x(-1), at_z(1), at_z(-1), partner, before, after]
    greeted += [at_line(j) for j in (1, 2, 3)]
    greeted += [at_zh(j) for j in (1, 2, 3)]
    greeted += [at_y(j) for j in (1, 2, 3)]
    barrier = pltpu.get_barrier_semaphore()
    for other in greeted:
        pl.semaphore_signal(barrier, inc=1, device_id=other, device_id_type=MESH)
    pl.semaphore_wait(barrier, len(greeted))

    started = []

    def send(src, dst, send_sem, recv_sem, device):
        copy = pltpu.make_async_remote_copy(
            src_ref=src, dst_ref=dst, send_sem=send_sem, recv_sem=recv_sem,
            device_id=device, device_id_type=MESH,
        )
        copy.start()
        started.append(copy)
        return copy

    halo_copy = send(
        frames_ref.at[pl.ds(0, HALO)], halo, h_send, h_recv, before
    )

    shard_of = [(w4_ref, 0), (w4_ref, 1), (w4_ref, 2), (w5_ref, 0), (w5_ref, 1),
                (w5_ref, 2), (w6_ref, 0), (w6_ref, 1), (w7_ref, 0), (w7_ref, 1)]
    flows = [[None] * 7 for _ in range(N_TAPS)]
    own_copies = []

    def own_slot(k):
        return wbuf.at[k, xi, core, zl]

    def own_block(k):
        ref, tap = shard_of[k]
        return ref.at[tap]

    def first(k, by):
        return at_z(by) if k % 2 == 0 else at_x(by)

    def second(k, by):
        return at_x(by) if k % 2 == 0 else at_z(by)

    def stage0(k):
        mine = pltpu.make_async_copy(own_block(k), own_slot(k), local_sem.at[k])
        mine.start()
        own_copies.append(mine)
        for j, by in ((0, 1), (1, -1)):
            flows[k][j] = send(own_block(k), own_slot(k), w_send.at[k, j],
                               w_recv.at[k, j], first(k, by))

    def stage1(k):
        flows[k][0].wait_recv()
        flows[k][1].wait_recv()
        if k % 2 == 0:
            block = wbuf.at[k, xi, core, lax.rem(zl - direction + 4, 4)]
        else:
            block = wbuf.at[k, lax.rem(xi - direction + 4, 4), core, zl]
        flows[k][2] = send(block, block, w_send.at[k, 2], w_recv.at[k, 2],
                           first(k, direction))

    def column(k, by):
        if k % 2 == 0:
            return wbuf.at[k, lax.rem(xi + by + 4, 4), core]
        return wbuf.at[k, :, core, lax.rem(zl + by + 4, 4)]

    def stage2(k):
        flows[k][2].wait_recv()
        own_copies[k].wait()
        for j, by in ((3, 1), (4, -1)):
            flows[k][j] = send(column(k, 0), column(k, 0), w_send.at[k, j],
                               w_recv.at[k, j], second(k, by))

    def stage3(k):
        flows[k][3].wait_recv()
        flows[k][4].wait_recv()
        block = column(k, -direction)
        flows[k][5] = send(block, block, w_send.at[k, 5], w_recv.at[k, 5],
                           second(k, direction))

    def stage4(k):
        flows[k][5].wait_recv()
        block = wbuf.at[k, :, core]
        flows[k][6] = send(block, block, w_send.at[k, 6], w_recv.at[k, 6], partner)

    def stage5(k):
        flows[k][6].wait_recv()

    stages = (stage0, stage1, stage2, stage3, stage4, stage5)

    pos_flows = [None] * 7
    pos_slot = pbuf.at[lax.rem(xi, 2), core, zl, xi // 2]

    def pos0():
        mine = pltpu.make_async_copy(pos_ref, pos_slot, local_sem.at[N_TAPS])
        mine.start()
        own_copies.append(mine)
        for j in range(3):
            pos_flows[j] = send(pos_ref, pos_slot, p_send.at[j], p_recv.at[j],
                                at_line(j + 1))

    def pos_column(by):
        x = lax.rem(xi + by + 4, 4)
        return pbuf.at[lax.rem(x, 2), core, :, x // 2]

    def pos1():
        for j in range(3):
            pos_flows[j].wait_recv()
        own_copies[-1].wait()
        for j, by in ((3, 1), (4, -1)):
            pos_flows[j] = send(pos_column(0), pos_column(0), p_send.at[j],
                                p_recv.at[j], at_x(by))

    def pos2():
        pos_flows[3].wait_recv()
        pos_flows[4].wait_recv()
        block = pos_column(-direction)
        pos_flows[5] = send(block, block, p_send.at[5], p_recv.at[5], at_x(direction))

    def pos3():
        pos_flows[5].wait_recv()
        block = pbuf.at[:, core]
        pos_flows[6] = send(block, block, p_send.at[6], p_recv.at[6], partner)

    def pos4():
        pos_flows[6].wait_recv()

    length = len_ref[0]

    def masked(block, base):
        rows = block.shape[0]
        index = base + lax.broadcasted_iota(jnp.int32, (rows, CH), 0)
        kept = jnp.where(index * 20 < length, block.astype(jnp.float32), 0.0)
        return kept

    def prepare():
        put(x4, 0, masked(frames_ref[...], tm * CH))
        put(x4, CH + HALO, jnp.zeros((32, CH), jnp.float32))
        hf[...] = jnp.zeros(hf.shape, jnp.float32)

    def prepare_halo():
        halo_copy.wait_recv()
        put(x4, CH, masked(halo[...], tm * CH + CH))

    def conv(x_ref, k, taps, rows):
        total = None
        for tap in range(taps):
            picked = jnp.concatenate(
                [x_ref[b, pl.ds(tap, rows, stride=2), :] for b in range(4)], axis=1
            ).astype(jnp.bfloat16)
            weight = wbuf[k + tap].reshape(CH, CH)
            part = jnp.dot(picked, weight, preferred_element_type=jnp.float32)
            total = part if total is None else total + part
        return gelu(norm(total)).astype(jnp.bfloat16).astype(jnp.float32)

    def put(x_ref, start, value):
        for b in range(4):
            x_ref[b, pl.ds(start, value.shape[0]), :] = value[:, b * 128 : b * 128 + 128]

    def layer4():
        prepare_halo()
        put(x5, 0, conv(x4, 0, 3, ROWS4))

    def layer5():
        put(x6, 0, conv(x5, 3, 3, 128))

    def layer6():
        put(x7, 0, conv(x6, 6, 2, 64))

    zh_flows = []

    def layer7():
        last = conv(x7, 8, 2, 32)
        normed = norm(last) * gain_ref[...] + nbias_ref[...]
        nbuf[tm] = normed.astype(jnp.bfloat16)
        block = nbuf.at[tm]
        for j in range(3):
            zh_flows.append(send(block, block, a_send.at[j], a_recv.at[j], at_zh(j + 1)))

    compute_after = {1: layer4, 2: layer5, 3: layer6, 4: layer7}
    n_groups = len(GROUPS_OF_TAPS)
    pos_at = {4: pos0, 7: pos1, 9: pos2}
    for step in range(n_groups + 5):
        for stage in range(5, -1, -1):
            group = step - stage
            if 0 <= group < n_groups:
                for k in GROUPS_OF_TAPS[group]:
                    stages[stage](k)
        if step in pos_at:
            pos_at[step]()
        if step == 1:
            prepare()
        done = step - 5
        if done in compute_after:
            compute_after[done]()

    y_flows = []
    for j in range(4):
        source = lax.rem(zh - j + 4, 4) * 4 + y
        if j:
            zh_flows[j - 1].wait_recv()
        block = nbuf.at[source]
        for by in (1, 2, 3):
            slot = 3 + j * 3 + by - 1
            y_flows.append(send(block, block, a_send.at[slot], a_recv.at[slot], at_y(by)))
    pos3()
    for copy in y_flows:
        copy.wait_recv()

    gathered = nbuf[...].reshape(CH, CH)
    hidden = jnp.dot(gathered, pw_ref[...], preferred_element_type=jnp.float32)
    hidden = (hidden + pb_ref[...].astype(jnp.float32)).astype(jnp.bfloat16)
    frame = lax.broadcasted_iota(jnp.int32, (CH, GW), 0)
    hidden = jnp.where(frame * 320 < length, hidden.astype(jnp.float32), 0.0)
    hf[pl.ds(64, CH), pl.ds(0, GW)] = hidden
    for tap in range(16):
        x16[:, pl.ds(tap * 128, 128)] = hf[pl.ds(tap, 624), :].astype(jnp.bfloat16)
    pos4()
    total = None
    for m in range(4):
        weight = jnp.concatenate(
            [pbuf[m // 2, m % 2, q].reshape(256, 512) for q in range(4)], axis=1
        )
        part = lax.dot_general(
            x16[pl.ds(16 * m, 576), :], weight, (((1,), (1,)), ((), ())),
            preferred_element_type=jnp.float32,
        )
        total = part if total is None else total + part
    conv_out = total[:CH, :128] + total[64:, 128:]
    position = gelu(conv_out[:, :GW] + posb_ref[...])
    encoded = hf[pl.ds(64, CH), pl.ds(0, GW)] + position
    out_ref[...] = encoded.T.astype(jnp.bfloat16)
    for copy in started:
        copy.wait_send()


def local(
    frames, lengths, fourth_conv, fifth_conv, sixth_conv, seventh_conv,
    norm_gain, norm_bias, project_weight, project_bias, position_weight, position_bias,
):
    taps = position_weight.reshape(4, GW, GW).transpose(1, 0, 2)
    taps = jnp.pad(taps, ((0, 8), (0, 0), (0, 8))).reshape(128, 512)
    vmem = pl.BlockSpec(memory_space=pltpu.VMEM)
    dma = pltpu.SemaphoreType.DMA
    out = pl.pallas_call(
        kernel,
        out_shape=jax.ShapeDtypeStruct((GW, CH), jnp.bfloat16),
        in_specs=[pl.BlockSpec(memory_space=pltpu.SMEM)] + [vmem] * 11,
        out_specs=vmem,
        scratch_shapes=[
            pltpu.VMEM((N_TAPS, 4, 2, 4, 16, CH), jnp.bfloat16),
            pltpu.VMEM((2, 2, 4, 2, 128, 512), jnp.bfloat16),
            pltpu.VMEM((HALO, CH), jnp.bfloat16),
            pltpu.VMEM((4, CH + HALO + 32, 128), jnp.float32),
            pltpu.VMEM((4, ROWS4, 128), jnp.float32),
            pltpu.VMEM((4, 128, 128), jnp.float32),
            pltpu.VMEM((4, 64, 128), jnp.float32),
            pltpu.VMEM((16, 32, CH), jnp.bfloat16),
            pltpu.VMEM((640, 128), jnp.float32),
            pltpu.VMEM((624, 2048), jnp.bfloat16),
            dma((N_TAPS + 1,)),
            dma((N_TAPS, 7)),
            dma((N_TAPS, 7)),
            dma((7,)),
            dma((7,)),
            dma((15,)),
            dma((15,)),
            dma,
            dma,
        ],
        compiler_params=pltpu.CompilerParams(
            collective_id=0, has_side_effects=True, vmem_limit_bytes=60 * 1024 * 1024
        ),
    )(
        lengths, frames[0], fourth_conv, fifth_conv, sixth_conv, seventh_conv,
        norm_gain.reshape(1, CH), norm_bias.reshape(1, CH),
        project_weight, project_bias, taps, position_bias.reshape(1, GW),
    )
    return out[None]


def solution(mesh):
    in_specs = (
        P(("section", "dp"), "tm", None),
        P(("section", "dp")),
        P(None, ("section", "dp"), None),
        P(None, ("section", "dp"), None),
        P(None, ("section", "dp"), None),
        P(None, ("section", "dp"), None),
        P(),
        P(),
        P(None, "tm"),
        P(None, "tm"),
        P("tm", ("section", "dp"), None),
        P("tm"),
    )
    out_specs = P(("section", "dp"), "tm", None)
    return jax.shard_map(local, mesh=mesh, in_specs=in_specs, out_specs=out_specs, check_vma=False)
```

```python
import jax
import jax.numpy as jnp
from jax import lax
from jax.experimental import pallas as pl
from jax.experimental.pallas import tpu as pltpu
from jax.sharding import PartitionSpec as P

MESH = pl.DeviceIdType.MESH
CH = 512
GW = 120
EPS = 1e-05
HALO = 16
ROWS4 = 272
N_TAPS = 10
WINDOW = 4
LAG4 = 2
LAG5 = 4


def norm(values):
    average = jnp.mean(values, axis=-1, keepdims=True)
    centred = values - average
    spread = jnp.mean(centred * centred, axis=-1, keepdims=True)
    return centred * lax.rsqrt(spread + EPS)


def gelu(values):
    return 0.5 * values * (1.0 + lax.erf(values * 0.7071067811865476))


def kernel(
    len_ref, frames_ref, w4_ref, w5_ref, w6_ref, w7_ref, gain_ref, nbias_ref,
    pw_ref, pb_ref, pos_ref, posb_ref, out_ref,
    wbuf, pbuf, fbuf, qbuf, pwbuf, halo, x4, x5, x6, x7, nbuf, hf, x16, relay32,
    local_sem, w_send, w_recv, p_send, p_recv, a_send, a_recv, h_send, h_recv, rounds,
):
    section = lax.axis_index("section")
    tm = lax.axis_index("tm")
    zl = lax.axis_index("dp")
    xi = section // 2
    core = lax.rem(section, 2)
    zh = tm // 4
    y = lax.rem(tm, 4)
    direction = 1 - 2 * core

    def at_x(by):
        return (lax.rem(xi + by + 4, 4) * 2 + core, tm, zl)

    def at_z(by):
        z = lax.rem(zh * 4 + zl + by + 16, 16)
        return (section, (z // 4) * 4 + y, lax.rem(z, 4))

    def at_line(by):
        return (section, tm, lax.rem(zl + by, 4))

    def at_zh(by):
        return (section, lax.rem(zh + by, 4) * 4 + y, zl)

    def at_y(by):
        return (section, zh * 4 + lax.rem(y + by + 4, 4), zl)

    partner = (xi * 2 + 1 - core, tm, zl)
    before = (section, lax.rem(tm + 15, 16), zl)

    def signal(sem, others):
        for other in others:
            pl.semaphore_signal(sem, inc=1, device_id=other, device_id_type=MESH)

    barrier = pltpu.get_barrier_semaphore()
    near = [partner, at_x(1), at_x(-1), at_z(1), at_z(-1), at_y(1), at_y(-1)]
    signal(barrier, near)

    fetches = []

    def fetch(src, dst):
        copy = pltpu.make_async_copy(src, dst, local_sem.at[len(fetches)])
        copy.start()
        fetches.append(copy)

    fetch(w4_ref, wbuf.at[pl.ds(0, 3), xi, core, zl])
    fetch(w5_ref, wbuf.at[pl.ds(3, 3), xi, core, zl])
    fetch(w6_ref, wbuf.at[pl.ds(6, 2), xi, core, zl])
    fetch(w7_ref, wbuf.at[pl.ds(8, 2), xi, core, zl])
    fetch(frames_ref, fbuf)
    fetch(pos_ref, qbuf)
    fetch(pw_ref, pwbuf)

    started = []

    def send(src, dst, send_sem, recv_sem, device):
        copy = pltpu.make_async_remote_copy(
            src_ref=src, dst_ref=dst, send_sem=send_sem, recv_sem=recv_sem,
            device_id=device, device_id_type=MESH,
        )
        copy.start()
        started.append(copy)
        return copy

    flows = [[None] * 7 for _ in range(N_TAPS)]

    def own(k):
        return wbuf.at[k, xi, core, zl]

    def first(k, by):
        return at_z(by) if k % 2 == 0 else at_x(by)

    def second(k, by):
        return at_x(by) if k % 2 == 0 else at_z(by)

    def flow(k, j, block, device):
        flows[k][j] = send(block, block, w_send.at[k, j], w_recv.at[k, j], device)

    def stage0(k):
        flow(k, 0, own(k), first(k, 1))
        flow(k, 1, own(k), first(k, -1))

    def stage1(k):
        flows[k][0].wait_recv()
        flows[k][1].wait_recv()
        if k % 2 == 0:
            block = wbuf.at[k, xi, core, lax.rem(zl - direction + 4, 4)]
        else:
            block = wbuf.at[k, lax.rem(xi - direction + 4, 4), core, zl]
        flow(k, 2, block, first(k, direction))

    def column(k, by):
        if k % 2 == 0:
            return wbuf.at[k, lax.rem(xi + by + 4, 4), core]
        return wbuf.at[k, :, core, lax.rem(zl + by + 4, 4)]

    def stage2(k):
        flows[k][2].wait_recv()
        flow(k, 3, column(k, 0), second(k, 1))
        flow(k, 4, column(k, 0), second(k, -1))

    def stage3(k):
        flows[k][3].wait_recv()
        flows[k][4].wait_recv()
        flow(k, 5, column(k, -direction), second(k, direction))

    def stage4(k):
        flows[k][5].wait_recv()
        flow(k, 6, wbuf.at[k, :, core], partner)

    def stage5(k):
        flows[k][6].wait_recv()

    pos_flows = {}

    def pos_block(x, z):
        return pbuf.at[lax.rem(x, 2), core, z, x // 2, pl.ds(0, GW)]

    def pos_send(name, block, device):
        j = len(pos_flows)
        pos_flows[name] = send(block, block, p_send.at[j], p_recv.at[j], device)

    def arrange_pos():
        values = qbuf[...].astype(jnp.float32)
        values = jnp.concatenate([values, jnp.zeros((4, 64), jnp.float32)], axis=1)
        for o in range(GW):
            relay32[pl.ds(o, 4, stride=128), :] = values[:, o * GW : o * GW + 128]
        for tap in range(4):
            pbuf[lax.rem(xi, 2), core, zl, xi // 2, :, pl.ds(tap * 128, 128)] = (
                relay32[pl.ds(tap * 128, 128), :].astype(jnp.bfloat16)
            )

    def pos_start():
        for j in (1, 2, 3):
            pos_send(("z", j), pos_block(xi, zl), at_line(j))
        pos_send(("x", 0, 1), pos_block(xi, zl), at_x(1))
        pos_send(("x", 0, -1), pos_block(xi, zl), at_x(-1))

    def pos_forward(j):
        pos_flows["z", j].wait_recv()
        block = pos_block(xi, lax.rem(zl - j + 4, 4))
        pos_send(("x", j, 1), block, at_x(1))
        pos_send(("x", j, -1), block, at_x(-1))

    def pos_relay(j):
        pos_flows["x", j, 1].wait_recv()
        pos_flows["x", j, -1].wait_recv()
        block = pos_block(lax.rem(xi - direction + 4, 4), lax.rem(zl - j + 4, 4))
        pos_send(("r", j), block, at_x(direction))

    def pos_swap(j):
        pos_flows["r", j].wait_recv()
        z = lax.rem(zl - j + 4, 4)
        block = pbuf.at[:, core, z, :, pl.ds(0, GW)]
        pos_send(("p", j), block, partner)

    length = len_ref[0]

    def masked(block, base):
        rows = block.shape[0]
        index = base + lax.broadcasted_iota(jnp.int32, (rows, CH), 0)
        return jnp.where(index * 20 < length, block.astype(jnp.float32), 0.0)

    def put(x_ref, start, value):
        for b in range(4):
            x_ref[b, pl.ds(start, value.shape[0]), :] = value[:, b * 128 : b * 128 + 128]

    def conv(x_ref, k, taps, rows):
        total = None
        for tap in range(taps):
            picked = jnp.concatenate(
                [x_ref[b, pl.ds(tap, rows, stride=2), :] for b in range(4)], axis=1
            ).astype(jnp.bfloat16)
            weight = wbuf[k + tap].reshape(CH, CH)
            part = jnp.dot(picked, weight, preferred_element_type=jnp.float32)
            total = part if total is None else total + part
        return gelu(norm(total)).astype(jnp.bfloat16).astype(jnp.float32)

    hf[...] = jnp.zeros(hf.shape, jnp.float32)
    put(x4, CH + HALO, jnp.zeros((32, CH), jnp.float32))
    for j in range(4):
        fetches[j].wait()
    pl.semaphore_wait(barrier, len(near))

    for k in range(N_TAPS):
        stage0(k)
    signal(rounds.at[0], [at_z(1), at_z(-1), at_y(1), at_y(-1)])
    fetches[4].wait()
    put(x4, 0, masked(fbuf[...], tm * CH))
    for k in range(N_TAPS):
        stage1(k)
        if k == 4:
            pl.semaphore_wait(rounds.at[0], 4)
            signal(rounds.at[1], [at_z(2), at_z(-2)])
    for k in range(WINDOW):
        stage2(k)
    pl.semaphore_wait(rounds.at[1], 2)
    signal(rounds.at[2], [at_z(4), at_z(-4)])
    fetches[5].wait()
    arrange_pos()
    pl.semaphore_wait(rounds.at[2], 2)
    halo_copy = send(frames_ref.at[pl.ds(0, HALO)], halo, h_send, h_recv, before)

    for step in range(N_TAPS + LAG5):
        if step < N_TAPS:
            stage3(step)
        if step + WINDOW < N_TAPS:
            stage2(step + WINDOW)
        if step == N_TAPS - 1:
            pos_start()
        if 0 <= step - LAG4 < N_TAPS:
            stage4(step - LAG4)
        done = step - LAG5
        if done >= 0:
            stage5(done)
            if done == 2:
                halo_copy.wait_recv()
                put(x4, CH, masked(halo[...], tm * CH + CH))
                put(x5, 0, conv(x4, 0, 3, ROWS4))
            if done == 5:
                put(x6, 0, conv(x5, 3, 3, 128))
            if done == 7:
                put(x7, 0, conv(x6, 6, 2, 64))
    last = conv(x7, 8, 2, 32)
    normed = norm(last) * gain_ref[...] + nbias_ref[...]
    nbuf[tm] = normed.astype(jnp.bfloat16)

    act_flows = {}

    def act_send(name, block, device):
        j = len(act_flows)
        act_flows[name] = send(block, block, a_send.at[j], a_recv.at[j], device)

    for j in (1, 3, 2):
        act_send(("z", j), nbuf.at[tm], at_zh(j))
    for by in (1, 2, 3):
        act_send(("y", 0, by), nbuf.at[tm], at_y(by))
    pos_relay(0)
    for j in (1, 2, 3):
        pos_forward(j)
    for j in (1, 3, 2):
        act_flows["z", j].wait_recv()
        block = nbuf.at[lax.rem(zh - j + 4, 4) * 4 + y]
        for by in (1, 2, 3):
            act_send(("y", j, by), block, at_y(by))
    pos_swap(0)
    for j in (1, 2, 3):
        pos_relay(j)
    fetches[6].wait()
    for j in range(4):
        for by in (1, 2, 3):
            act_flows["y", j, by].wait_recv()

    gathered = nbuf[...].reshape(CH, CH)
    hidden = lax.dot_general(
        gathered, pwbuf[...], (((1,), (1,)), ((), ())), preferred_element_type=jnp.float32
    )
    hidden = (hidden + pb_ref[...].astype(jnp.float32)).astype(jnp.bfloat16)
    frame = lax.broadcasted_iota(jnp.int32, (CH, GW), 0)
    hidden = jnp.where(frame * 320 < length, hidden.astype(jnp.float32), 0.0)
    hf[pl.ds(64, CH), pl.ds(0, GW)] = hidden
    for j in (1, 2, 3):
        pos_swap(j)
    for tap in range(16):
        x16[:, pl.ds(tap * 128, 128)] = hf[pl.ds(tap, 624), :].astype(jnp.bfloat16)
    for j in range(4):
        pos_flows["p", j].wait_recv()
    total = None
    for m in range(4):
        weight = jnp.concatenate(
            [pbuf[m // 2, m % 2, q].reshape(256, 512) for q in range(4)], axis=1
        )
        part = lax.dot_general(
            x16[pl.ds(16 * m, 576), :], weight, (((1,), (1,)), ((), ())),
            preferred_element_type=jnp.float32,
        )
        total = part if total is None else total + part
    conv_out = total[:CH, :128] + total[64:, 128:]
    position = gelu(conv_out[:, :GW] + posb_ref[...])
    encoded = hf[pl.ds(64, CH), pl.ds(0, GW)] + position
    out_ref[...] = encoded.T.astype(jnp.bfloat16)
    for copy in started:
        copy.wait_send()


def local(
    frames, lengths, fourth_conv, fifth_conv, sixth_conv, seventh_conv,
    norm_gain, norm_bias, project_weight, project_bias, position_weight, position_bias,
):
    vmem = pl.BlockSpec(memory_space=pltpu.VMEM)
    hbm = pl.BlockSpec(memory_space=pl.ANY)
    smem = pl.BlockSpec(memory_space=pltpu.SMEM)
    dma = pltpu.SemaphoreType.DMA
    out = pl.pallas_call(
        kernel,
        out_shape=jax.ShapeDtypeStruct((GW, CH), jnp.bfloat16),
        in_specs=[smem, hbm, hbm, hbm, hbm, hbm, vmem, vmem, hbm, vmem, hbm, vmem],
        out_specs=vmem,
        scratch_shapes=[
            pltpu.VMEM((N_TAPS, 4, 2, 4, 16, CH), jnp.bfloat16),
            pltpu.VMEM((2, 2, 4, 2, 128, 512), jnp.bfloat16),
            pltpu.VMEM((CH, CH), jnp.bfloat16),
            pltpu.VMEM((4, GW * GW), jnp.bfloat16),
            pltpu.VMEM((GW, CH), jnp.bfloat16),
            pltpu.VMEM((HALO, CH), jnp.bfloat16),
            pltpu.VMEM((4, CH + HALO + 32, 128), jnp.float32),
            pltpu.VMEM((4, ROWS4, 128), jnp.float32),
            pltpu.VMEM((4, 128, 128), jnp.float32),
            pltpu.VMEM((4, 64, 128), jnp.float32),
            pltpu.VMEM((16, 32, CH), jnp.bfloat16),
            pltpu.VMEM((640, 128), jnp.float32),
            pltpu.VMEM((624, 2048), jnp.bfloat16),
            pltpu.VMEM((512, 128), jnp.float32),
            dma((7,)),
            dma((N_TAPS, 7)),
            dma((N_TAPS, 7)),
            dma((19,)),
            dma((19,)),
            dma((15,)),
            dma((15,)),
            dma,
            dma,
            pltpu.SemaphoreType.REGULAR((3,)),
        ],
        compiler_params=pltpu.CompilerParams(
            collective_id=0, has_side_effects=True, vmem_limit_bytes=60 * 1024 * 1024
        ),
    )(
        lengths, frames[0], fourth_conv, fifth_conv, sixth_conv, seventh_conv,
        norm_gain.reshape(1, CH), norm_bias.reshape(1, CH),
        project_weight.T, project_bias, position_weight[0], position_bias.reshape(1, GW),
    )
    return out[None]


def solution(mesh):
    in_specs = (
        P(("section", "dp"), "tm", None),
        P(("section", "dp")),
        P(None, ("section", "dp"), None),
        P(None, ("section", "dp"), None),
        P(None, ("section", "dp"), None),
        P(None, ("section", "dp"), None),
        P(),
        P(),
        P(None, "tm"),
        P(None, "tm"),
        P("tm", ("section", "dp"), None),
        P("tm"),
    )
    out_specs = P(("section", "dp"), "tm", None)
    return jax.shard_map(local, mesh=mesh, in_specs=in_specs, out_specs=out_specs, check_vma=False)
```

```python
import jax
import jax.numpy as jnp
from jax import lax
from jax.experimental import pallas as pl
from jax.experimental.pallas import tpu as pltpu
from jax.sharding import PartitionSpec as P

MESH = pl.DeviceIdType.MESH
CH = 512
GW = 120
EPS = 1e-05
HALO = 16
ROWS4 = 272
N_TAPS = 10
PLAIN = 6


def norm(values):
    average = jnp.mean(values, axis=-1, keepdims=True)
    centred = values - average
    spread = jnp.mean(centred * centred, axis=-1, keepdims=True)
    return centred * lax.rsqrt(spread + EPS)


def gelu(values):
    return 0.5 * values * (1.0 + lax.erf(values * 0.7071067811865476))


def kernel(
    len_ref, frames_ref, w4_ref, w5_ref, w6_ref, w7_ref, gain_ref, nbias_ref,
    pw_ref, pb_ref, pos_ref, posb_ref, out_ref,
    wbuf, stage, pbuf, fbuf, qbuf, pwbuf, bbuf, halo, x4, x5, x6, x7, nbuf, sbuf, hbuf, hf, x16, relay32,
    local_sem, w_send, w_recv, p_send, p_recv, a_send, a_recv, h_send, h_recv, rounds,
):
    section = lax.axis_index("section")
    tm = lax.axis_index("tm")
    zl = lax.axis_index("dp")
    xi = section // 2
    core = lax.rem(section, 2)
    zh = tm // 4
    y = lax.rem(tm, 4)
    direction = 1 - 2 * core

    def at_x(by):
        return (lax.rem(xi + by + 4, 4) * 2 + core, tm, zl)

    def at_z(by):
        z = lax.rem(zh * 4 + zl + by + 16, 16)
        return (section, (z // 4) * 4 + y, lax.rem(z, 4))

    def at_line(by):
        return (section, tm, lax.rem(zl + by, 4))

    def at_zh(by):
        return (section, lax.rem(zh + by, 4) * 4 + y, zl)

    def at_y(by):
        return (section, zh * 4 + lax.rem(y + by + 4, 4), zl)

    partner = (xi * 2 + 1 - core, tm, zl)
    before = (section, lax.rem(tm + 15, 16), zl)

    def signal(sem, others):
        for other in others:
            pl.semaphore_signal(sem, inc=1, device_id=other, device_id_type=MESH)

    def at_plane(dx, dz):
        by = dz * direction if dz == 2 else dz
        z = lax.rem(zh * 4 + zl + by + 16, 16)
        return (lax.rem(xi + dx + 4, 4) * 2 + core, (z // 4) * 4 + y, lax.rem(z, 4))

    barrier = pltpu.get_barrier_semaphore()
    beside = [at_x(1), at_x(-1), at_z(1), at_z(-1), at_y(1), at_y(-1)]
    signal(barrier, beside + [partner])

    fetches = []

    def fetch(src, dst):
        copy = pltpu.make_async_copy(src, dst, local_sem.at[len(fetches)])
        copy.start()
        fetches.append(copy)

    fetch(w4_ref, wbuf.at[pl.ds(0, 3), xi, core, zl])
    fetch(w5_ref, wbuf.at[pl.ds(3, 3), xi, core, zl])
    fetch(w6_ref, stage.at[pl.ds(0, 2)])
    fetch(w7_ref, stage.at[pl.ds(2, 2)])
    fetch(frames_ref, fbuf)
    fetch(pos_ref, qbuf)
    fetch(pw_ref, pwbuf.at[y])

    started = []

    def send(src, dst, send_sem, recv_sem, device):
        copy = pltpu.make_async_remote_copy(
            src_ref=src, dst_ref=dst, send_sem=send_sem, recv_sem=recv_sem,
            device_id=device, device_id_type=MESH,
        )
        copy.start()
        started.append(copy)
        return copy

    flows = {}

    def flow(name, block, device):
        j = len(flows)
        flows[name] = send(block, block, w_send.at[j], w_recv.at[j], device)

    def own(k):
        return wbuf.at[k, xi, core, zl]

    def stage0(k, by):
        device = at_plane(0, by) if k % 2 == 0 else at_plane(by, 0)
        flow(("a", k, by), own(k), device)

    def line(k, by):
        if k % 2 == 0:
            return wbuf.at[k, lax.rem(xi + by + 4, 4), core]
        return wbuf.at[k, :, core, lax.rem(zl + by + 4, 4)]

    def second(k, by):
        return at_x(by) if k % 2 == 0 else at_z(by)

    def stage1(k):
        for by in (1, -1, 2):
            flows["a", k, by].wait_recv()
        flow(("b", k, 1), line(k, 0), second(k, 1))
        flow(("b", k, -1), line(k, 0), second(k, -1))

    def pass_on(k):
        flows["b", k, 1].wait_recv()
        flows["b", k, -1].wait_recv()
        flow(("b", k, 2), line(k, -direction), second(k, direction))

    def stage2(k):
        flows["b", k, 2].wait_recv()
        flow(("p", k), wbuf.at[k, :, core], partner)

    shared = PLAIN + y

    def share0(dx, dz):
        j = len(flows)
        flows["s", dx, dz] = send(
            stage.at[y], wbuf.at[shared, xi, core, zl], w_send.at[j], w_recv.at[j],
            at_plane(dx, dz),
        )

    def lend(by):
        flow(("w", by), pwbuf.at[y], at_y(by))
        flow(("c", by), bbuf.at[y], at_y(by))

    def share1(dx):
        for dz in (0, 1, -1, 2):
            if (dx, dz) != (0, 0):
                flows["s", dx, dz].wait_recv()
        block = wbuf.at[shared, lax.rem(xi - dx + 4, 4), core]
        for by in (1, 3, 2):
            flow(("y", dx, by), block, at_y(by))

    def share2(by):
        for dx in (0, 1, -1, 2):
            flows["y", dx, by].wait_recv()
        flow(("q", by), wbuf.at[PLAIN + lax.rem(y - by + 4, 4), :, core], partner)

    pos_flows = {}

    def pos_block(x, z):
        return pbuf.at[lax.rem(x, 2), core, z, x // 2, pl.ds(0, GW)]

    def pos_send(name, block, device):
        j = len(pos_flows)
        pos_flows[name] = send(block, block, p_send.at[j], p_recv.at[j], device)

    def arrange_pos():
        values = qbuf[...].astype(jnp.float32)
        values = jnp.concatenate([values, jnp.zeros((4, 64), jnp.float32)], axis=1)
        for o in range(GW):
            relay32[pl.ds(o, 4, stride=128), :] = values[:, o * GW : o * GW + 128]
        for tap in range(4):
            pbuf[lax.rem(xi, 2), core, zl, xi // 2, :, pl.ds(tap * 128, 128)] = (
                relay32[pl.ds(tap * 128, 128), :].astype(jnp.bfloat16)
            )

    def pos_start():
        for j in (1, 2, 3):
            pos_send(("z", j), pos_block(xi, zl), at_line(j))
        pos_send(("x", 0, 1), pos_block(xi, zl), at_x(1))
        pos_send(("x", 0, -1), pos_block(xi, zl), at_x(-1))

    def pos_forward(j):
        pos_flows["z", j].wait_recv()
        block = pos_block(xi, lax.rem(zl - j + 4, 4))
        pos_send(("x", j, 1), block, at_x(1))
        pos_send(("x", j, -1), block, at_x(-1))

    def pos_relay(j):
        pos_flows["x", j, 1].wait_recv()
        pos_flows["x", j, -1].wait_recv()
        block = pos_block(lax.rem(xi - direction + 4, 4), lax.rem(zl - j + 4, 4))
        pos_send(("r", j), block, at_x(direction))

    def pos_swap(j):
        pos_flows["r", j].wait_recv()
        z = lax.rem(zl - j + 4, 4)
        block = pbuf.at[:, core, z, :, pl.ds(0, GW)]
        pos_send(("p", j), block, partner)

    length = len_ref[0]

    def masked(block, base):
        rows = block.shape[0]
        index = base + lax.broadcasted_iota(jnp.int32, (rows, CH), 0)
        return jnp.where(index * 20 < length, block.astype(jnp.float32), 0.0)

    def put(x_ref, start, value):
        for b in range(4):
            x_ref[b, pl.ds(start, value.shape[0]), :] = value[:, b * 128 : b * 128 + 128]

    def conv(x_ref, k, taps, rows):
        total = None
        for tap in range(taps):
            picked = jnp.concatenate(
                [x_ref[b, pl.ds(tap, rows, stride=2), :] for b in range(4)], axis=1
            ).astype(jnp.bfloat16)
            weight = wbuf[k + tap].reshape(CH, CH)
            part = jnp.dot(picked, weight, preferred_element_type=jnp.float32)
            total = part if total is None else total + part
        return gelu(norm(total)).astype(jnp.bfloat16).astype(jnp.float32)

    bias = jnp.concatenate(
        [pb_ref[...].astype(jnp.float32), jnp.zeros((1, 128 - GW), jnp.float32)], axis=1
    )
    bbuf[y] = jnp.broadcast_to(bias, (16, 128)).astype(jnp.bfloat16)
    hf[...] = jnp.zeros(hf.shape, jnp.float32)
    put(x4, CH + HALO, jnp.zeros((32, CH), jnp.float32))
    for j in range(4):
        fetches[j].wait()
    fetch(stage.at[y], wbuf.at[PLAIN + y, xi, core, zl])
    pl.semaphore_wait(barrier, 7)
    signal(rounds.at[0], beside)

    share0(0, 1)
    share0(0, -1)
    for k in range(PLAIN):
        stage0(k, 1)
        stage0(k, -1)
    share0(1, 0)
    share0(-1, 0)
    pl.semaphore_wait(rounds.at[0], 6)
    signal(rounds.at[1], [at_z(2), at_z(-2), at_x(2)])
    share0(0, 2)
    for k in range(PLAIN):
        stage0(k, 2)
    for dx, dz in ((2, 0), (1, 1), (1, -1), (-1, 1), (-1, -1)):
        share0(dx, dz)
    fetches[4].wait()
    put(x4, 0, masked(fbuf[...], tm * CH))
    pl.semaphore_wait(rounds.at[1], 3)
    signal(rounds.at[2], [at_z(4), at_z(-4)])
    for dx, dz in ((1, 2), (-1, 2), (2, 1), (2, -1), (2, 2)):
        share0(dx, dz)
    fetches[5].wait()
    arrange_pos()
    fetches[7].wait()
    share1(0)
    for k in range(PLAIN):
        stage1(k)
    pl.semaphore_wait(rounds.at[2], 2)
    halo_copy = send(frames_ref.at[pl.ds(0, HALO)], halo, h_send, h_recv, before)
    pos_start()
    share1(1)
    share1(-1)
    pass_on(0)
    pass_on(1)
    share1(2)
    fetches[6].wait()
    for by in (1, 3, 2):
        lend(by)
    for k in range(2, PLAIN):
        pass_on(k)
    flow(("q", 0), wbuf.at[shared, :, core], partner)
    for k in range(PLAIN):
        stage2(k)
        if k == 4:
            for j in range(3):
                flows["p", j].wait_recv()
            halo_copy.wait_recv()
            put(x4, CH, masked(halo[...], tm * CH + CH))
            put(x5, 0, conv(x4, 0, 3, ROWS4))
    pos_forward(1)
    for by in (1, 3, 2):
        share2(by)
    pos_forward(2)
    for k in range(3, PLAIN):
        flows["p", k].wait_recv()
    put(x6, 0, conv(x5, 3, 3, 128))
    for by in (0, 1, 3, 2):
        flows["q", by].wait_recv()
    put(x7, 0, conv(x6, 6, 2, 64))
    last = conv(x7, 8, 2, 32)
    normed = norm(last) * gain_ref[...] + nbias_ref[...]
    nbuf[0] = normed.astype(jnp.bfloat16)

    act_flows = {}

    for j in (1, 3, 2):
        act_flows["z", j] = send(
            nbuf.at[0], nbuf.at[j], a_send.at[j - 1], a_recv.at[j - 1], at_zh(j)
        )
    for by in (1, 3, 2):
        flows["w", by].wait_recv()
        flows["c", by].wait_recv()
    row = lax.broadcasted_iota(jnp.int32, (32, GW), 0)

    def project(j):
        source = lax.rem(zh - j + 4, 4) * 4 + y
        rows = nbuf[j]
        for group in range(4):
            hidden = lax.dot_general(
                rows, pwbuf[group], (((1,), (1,)), ((), ())),
                preferred_element_type=jnp.float32,
            )
            hidden = hidden + bbuf[group, pl.ds(0, 1), pl.ds(0, GW)].astype(jnp.float32)
            hidden = jnp.where((source * 32 + row) * 320 < length, hidden, 0.0)
            hidden = jnp.concatenate([hidden, jnp.zeros((32, 128 - GW), jnp.float32)], axis=1)
            hidden = hidden.astype(jnp.bfloat16)
            sbuf[j, group] = hidden
            mine = hidden if group == 0 else jnp.where(group == y, hidden, mine)
        for by in (1, 3, 2):
            j_send = len(act_flows)
            act_flows["y", j, by] = send(
                sbuf.at[j, lax.rem(y + by, 4)], hbuf.at[source],
                a_send.at[j_send], a_recv.at[j_send], at_y(by),
            )
        hbuf[source] = mine

    project(0)
    pos_relay(0)
    pos_forward(3)
    pos_relay(1)
    pos_relay(2)
    pos_relay(3)
    for j in (1, 3, 2):
        act_flows["z", j].wait_recv()
        project(j)
    pos_swap(0)
    pos_swap(1)
    for j in range(4):
        for by in (1, 2, 3):
            act_flows["y", j, by].wait_recv()
    hf[pl.ds(64, CH), :] = hbuf[...].reshape(CH, 128).astype(jnp.float32)
    for tap in range(16):
        x16[:, pl.ds(tap * 128, 128)] = hf[pl.ds(tap, 624), :].astype(jnp.bfloat16)
    pos_swap(2)
    pos_swap(3)
    for j in range(4):
        pos_flows["p", j].wait_recv()
    total = None
    for m in range(4):
        weight = jnp.concatenate(
            [pbuf[m // 2, m % 2, q].reshape(256, 512) for q in range(4)], axis=1
        )
        part = lax.dot_general(
            x16[pl.ds(16 * m, 576), :], weight, (((1,), (1,)), ((), ())),
            preferred_element_type=jnp.float32,
        )
        total = part if total is None else total + part
    conv_out = total[:CH, :128] + total[64:, 128:]
    position = gelu(conv_out[:, :GW] + posb_ref[...])
    encoded = hf[pl.ds(64, CH), pl.ds(0, GW)] + position
    out_ref[...] = encoded.T.astype(jnp.bfloat16)
    for copy in started:
        copy.wait_send()


def local(
    frames, lengths, fourth_conv, fifth_conv, sixth_conv, seventh_conv,
    norm_gain, norm_bias, project_weight, project_bias, position_weight, position_bias,
):
    vmem = pl.BlockSpec(memory_space=pltpu.VMEM)
    hbm = pl.BlockSpec(memory_space=pl.ANY)
    smem = pl.BlockSpec(memory_space=pltpu.SMEM)
    dma = pltpu.SemaphoreType.DMA
    out = pl.pallas_call(
        kernel,
        out_shape=jax.ShapeDtypeStruct((GW, CH), jnp.bfloat16),
        in_specs=[smem, hbm, hbm, hbm, hbm, hbm, vmem, vmem, hbm, vmem, hbm, vmem],
        out_specs=vmem,
        scratch_shapes=[
            pltpu.VMEM((N_TAPS, 4, 2, 4, 16, CH), jnp.bfloat16),
            pltpu.VMEM((4, 16, CH), jnp.bfloat16),
            pltpu.VMEM((2, 2, 4, 2, 128, 512), jnp.bfloat16),
            pltpu.VMEM((CH, CH), jnp.bfloat16),
            pltpu.VMEM((4, GW * GW), jnp.bfloat16),
            pltpu.VMEM((4, GW, CH), jnp.bfloat16),
            pltpu.VMEM((4, 16, 128), jnp.bfloat16),
            pltpu.VMEM((HALO, CH), jnp.bfloat16),
            pltpu.VMEM((4, CH + HALO + 32, 128), jnp.float32),
            pltpu.VMEM((4, ROWS4, 128), jnp.float32),
            pltpu.VMEM((4, 128, 128), jnp.float32),
            pltpu.VMEM((4, 64, 128), jnp.float32),
            pltpu.VMEM((4, 32, CH), jnp.bfloat16),
            pltpu.VMEM((4, 4, 32, 128), jnp.bfloat16),
            pltpu.VMEM((16, 32, 128), jnp.bfloat16),
            pltpu.VMEM((640, 128), jnp.float32),
            pltpu.VMEM((624, 2048), jnp.bfloat16),
            pltpu.VMEM((512, 128), jnp.float32),
            dma((8,)),
            dma((79,)),
            dma((79,)),
            dma((19,)),
            dma((19,)),
            dma((15,)),
            dma((15,)),
            dma,
            dma,
            pltpu.SemaphoreType.REGULAR((3,)),
        ],
        compiler_params=pltpu.CompilerParams(
            collective_id=0, has_side_effects=True, vmem_limit_bytes=60 * 1024 * 1024
        ),
    )(
        lengths, frames[0], fourth_conv, fifth_conv, sixth_conv, seventh_conv,
        norm_gain.reshape(1, CH), norm_bias.reshape(1, CH),
        project_weight.T, project_bias, position_weight[0], position_bias.reshape(1, GW),
    )
    return out[None]


def solution(mesh):
    in_specs = (
        P(("section", "dp"), "tm", None),
        P(("section", "dp")),
        P(None, ("section", "dp"), None),
        P(None, ("section", "dp"), None),
        P(None, ("section", "dp"), None),
        P(None, ("section", "dp"), None),
        P(),
        P(),
        P(None, "tm"),
        P(None, "tm"),
        P("tm", ("section", "dp"), None),
        P("tm"),
    )
    out_specs = P(("section", "dp"), "tm", None)
    return jax.shard_map(local, mesh=mesh, in_specs=in_specs, out_specs=out_specs, check_vma=False)
```

```python
import jax
import jax.numpy as jnp
from jax import lax
from jax.experimental import pallas as pl
from jax.experimental.pallas import tpu as pltpu
from jax.sharding import PartitionSpec as P

MESH = pl.DeviceIdType.MESH
CH = 512
GW = 120
EPS = 1e-05
HALO = 16
ROWS4 = 272
N_TAPS = 10
PLAIN = 6


def norm(values):
    average = jnp.mean(values, axis=-1, keepdims=True)
    centred = values - average
    spread = jnp.mean(centred * centred, axis=-1, keepdims=True)
    return centred * lax.rsqrt(spread + EPS)


def gelu(values):
    return 0.5 * values * (1.0 + lax.erf(values * 0.7071067811865476))


def kernel(
    len_ref, frames_ref, w4_ref, w5_ref, w6_ref, w7_ref, gain_ref, nbias_ref,
    pw_ref, pb_ref, pos_ref, posb_ref, out_ref,
    wbuf, stage, pbuf, fbuf, qbuf, pwbuf, bbuf, halo, x4, x5, x6, x7, nbuf, sbuf, hbuf, hf, x16, relay32,
    local_sem, w_send, w_recv, p_send, p_recv, a_send, a_recv, h_send, h_recv, rounds,
):
    section = lax.axis_index("section")
    tm = lax.axis_index("tm")
    zl = lax.axis_index("dp")
    xi = section // 2
    core = lax.rem(section, 2)
    zh = tm // 4
    y = lax.rem(tm, 4)
    direction = 1 - 2 * core

    def at_x(by):
        return (lax.rem(xi + by + 4, 4) * 2 + core, tm, zl)

    def at_z(by):
        z = lax.rem(zh * 4 + zl + by + 16, 16)
        return (section, (z // 4) * 4 + y, lax.rem(z, 4))

    def at_line(by):
        return (section, tm, lax.rem(zl + by, 4))

    def at_zh(by):
        return (section, lax.rem(zh + by, 4) * 4 + y, zl)

    def at_y(by):
        return (section, zh * 4 + lax.rem(y + by + 4, 4), zl)

    partner = (xi * 2 + 1 - core, tm, zl)
    before = (section, lax.rem(tm + 15, 16), zl)

    def signal(sem, others):
        for other in others:
            pl.semaphore_signal(sem, inc=1, device_id=other, device_id_type=MESH)

    def at_plane(dx, dz):
        by = dz * direction if dz == 2 else dz
        z = lax.rem(zh * 4 + zl + by + 16, 16)
        return (lax.rem(xi + dx + 4, 4) * 2 + core, (z // 4) * 4 + y, lax.rem(z, 4))

    barrier = pltpu.get_barrier_semaphore()
    beside = [at_x(1), at_x(-1), at_z(1), at_z(-1), at_y(1), at_y(-1)]
    signal(barrier, beside + [partner])

    fetches = []

    def fetch(src, dst):
        copy = pltpu.make_async_copy(src, dst, local_sem.at[len(fetches)])
        copy.start()
        fetches.append(copy)

    fetch(w4_ref, wbuf.at[pl.ds(0, 3), xi, core, zl])
    fetch(w5_ref, wbuf.at[pl.ds(3, 3), xi, core, zl])
    fetch(w6_ref, stage.at[pl.ds(0, 2)])
    fetch(w7_ref, stage.at[pl.ds(2, 2)])
    fetch(frames_ref, fbuf)
    fetch(pos_ref, qbuf)
    fetch(pw_ref, pwbuf.at[y])

    started = []

    def send(src, dst, send_sem, recv_sem, device):
        copy = pltpu.make_async_remote_copy(
            src_ref=src, dst_ref=dst, send_sem=send_sem, recv_sem=recv_sem,
            device_id=device, device_id_type=MESH,
        )
        copy.start()
        started.append(copy)
        return copy

    flows = {}

    def flow(name, block, device):
        j = len(flows)
        flows[name] = send(block, block, w_send.at[j], w_recv.at[j], device)

    def own(k):
        return wbuf.at[k, xi, core, zl]

    def stage0(k, by):
        device = at_plane(0, by) if k % 2 == 0 else at_plane(by, 0)
        flow(("a", k, by), own(k), device)

    def line(k, by):
        if k % 2 == 0:
            return wbuf.at[k, lax.rem(xi + by + 4, 4), core]
        return wbuf.at[k, :, core, lax.rem(zl + by + 4, 4)]

    def second(k, by):
        return at_x(by) if k % 2 == 0 else at_z(by)

    def stage1(k):
        for by in (1, -1, 2):
            flows["a", k, by].wait_recv()
        flow(("b", k, 1), line(k, 0), second(k, 1))
        flow(("b", k, -1), line(k, 0), second(k, -1))

    def pass_on(k):
        flows["b", k, 1].wait_recv()
        flows["b", k, -1].wait_recv()
        flow(("b", k, 2), line(k, -direction), second(k, direction))

    def stage2(k):
        flows["b", k, 2].wait_recv()
        flow(("p", k), wbuf.at[k, :, core], partner)

    shared = PLAIN + y

    def share0(dx, dz):
        j = len(flows)
        flows["s", dx, dz] = send(
            stage.at[y], wbuf.at[shared, xi, core, zl], w_send.at[j], w_recv.at[j],
            at_plane(dx, dz),
        )

    def lend(by):
        flow(("w", by), pwbuf.at[y], at_y(by))
        flow(("c", by), bbuf.at[y], at_y(by))

    def share1(dx):
        for dz in (0, 1, -1, 2):
            if (dx, dz) != (0, 0):
                flows["s", dx, dz].wait_recv()
        block = wbuf.at[shared, lax.rem(xi - dx + 4, 4), core]
        for by in (1, 3, 2):
            flow(("y", dx, by), block, at_y(by))

    def share2(by):
        for dx in (0, 1, -1, 2):
            flows["y", dx, by].wait_recv()
        flow(("q", by), wbuf.at[PLAIN + lax.rem(y - by + 4, 4), :, core], partner)

    pos_flows = {}

    def pos_block(x, z):
        return pbuf.at[lax.rem(x, 2), core, z, x // 2, pl.ds(0, GW)]

    def pos_send(name, block, device):
        j = len(pos_flows)
        pos_flows[name] = send(block, block, p_send.at[j], p_recv.at[j], device)

    def arrange_pos():
        values = qbuf[...].astype(jnp.float32)
        values = jnp.concatenate([values, jnp.zeros((4, 64), jnp.float32)], axis=1)
        for o in range(GW):
            relay32[pl.ds(o, 4, stride=128), :] = values[:, o * GW : o * GW + 128]
        for tap in range(4):
            pbuf[lax.rem(xi, 2), core, zl, xi // 2, :, pl.ds(tap * 128, 128)] = (
                relay32[pl.ds(tap * 128, 128), :].astype(jnp.bfloat16)
            )

    def pos_start():
        for j in (1, 2, 3):
            pos_send(("z", j), pos_block(xi, zl), at_line(j))
        pos_send(("x", 0, 1), pos_block(xi, zl), at_x(1))
        pos_send(("x", 0, -1), pos_block(xi, zl), at_x(-1))

    def pos_forward(j):
        pos_flows["z", j].wait_recv()
        block = pos_block(xi, lax.rem(zl - j + 4, 4))
        pos_send(("x", j, 1), block, at_x(1))
        pos_send(("x", j, -1), block, at_x(-1))

    def pos_relay(j):
        pos_flows["x", j, 1].wait_recv()
        pos_flows["x", j, -1].wait_recv()
        block = pos_block(lax.rem(xi - direction + 4, 4), lax.rem(zl - j + 4, 4))
        pos_send(("r", j), block, at_x(direction))
        pos_share(j)

    def pos_share(j):
        for dx in (0, 1, -1):
            block = pos_block(lax.rem(xi + dx + 4, 4), lax.rem(zl - j + 4, 4))
            pos_send(("p", j, dx), block, partner)

    def pos_swap(j):
        pos_flows["r", j].wait_recv()
        block = pos_block(lax.rem(xi + 2, 4), lax.rem(zl - j + 4, 4))
        pos_send(("p", j, 2), block, partner)

    length = len_ref[0]

    def masked(block, base):
        rows = block.shape[0]
        index = base + lax.broadcasted_iota(jnp.int32, (rows, CH), 0)
        return jnp.where(index * 20 < length, block.astype(jnp.float32), 0.0)

    def put(x_ref, start, value):
        for b in range(4):
            x_ref[b, pl.ds(start, value.shape[0]), :] = value[:, b * 128 : b * 128 + 128]

    def conv(x_ref, k, taps, rows):
        total = None
        for tap in range(taps):
            picked = jnp.concatenate(
                [x_ref[b, pl.ds(tap, rows, stride=2), :] for b in range(4)], axis=1
            ).astype(jnp.bfloat16)
            weight = wbuf[k + tap].reshape(CH, CH)
            part = jnp.dot(picked, weight, preferred_element_type=jnp.float32)
            total = part if total is None else total + part
        return gelu(norm(total)).astype(jnp.bfloat16).astype(jnp.float32)

    bias = jnp.concatenate(
        [pb_ref[...].astype(jnp.float32), jnp.zeros((1, 128 - GW), jnp.float32)], axis=1
    )
    bbuf[y] = jnp.broadcast_to(bias, (16, 128)).astype(jnp.bfloat16)
    hf[...] = jnp.zeros(hf.shape, jnp.float32)
    put(x4, CH + HALO, jnp.zeros((32, CH), jnp.float32))
    for j in range(4):
        fetches[j].wait()
    fetch(stage.at[y], wbuf.at[PLAIN + y, xi, core, zl])
    pl.semaphore_wait(barrier, 7)
    signal(rounds.at[0], beside)

    share0(0, 1)
    share0(0, -1)
    for k in range(PLAIN):
        stage0(k, 1)
        stage0(k, -1)
    share0(1, 0)
    share0(-1, 0)
    pl.semaphore_wait(rounds.at[0], 6)
    signal(rounds.at[1], [at_z(2), at_z(-2), at_x(2)])
    share0(0, 2)
    for k in range(PLAIN):
        stage0(k, 2)
    for dx, dz in ((2, 0), (1, 1), (1, -1), (-1, 1), (-1, -1)):
        share0(dx, dz)
    fetches[4].wait()
    put(x4, 0, masked(fbuf[...], tm * CH))
    pl.semaphore_wait(rounds.at[1], 3)
    signal(rounds.at[2], [at_z(4), at_z(-4)])
    for dx, dz in ((1, 2), (-1, 2), (2, 1), (2, -1), (2, 2)):
        share0(dx, dz)
    fetches[5].wait()
    arrange_pos()
    fetches[7].wait()
    share1(0)
    for k in range(PLAIN):
        stage1(k)
    pl.semaphore_wait(rounds.at[2], 2)
    halo_copy = send(frames_ref.at[pl.ds(0, HALO)], halo, h_send, h_recv, before)
    pos_start()
    share1(1)
    share1(-1)
    pass_on(0)
    pass_on(1)
    share1(2)
    fetches[6].wait()
    for by in (1, 3, 2):
        lend(by)
    for k in range(2, PLAIN):
        pass_on(k)
    flow(("q", 0), wbuf.at[shared, :, core], partner)
    for k in range(PLAIN):
        stage2(k)
        if k == 4:
            for j in range(3):
                flows["p", j].wait_recv()
            halo_copy.wait_recv()
            put(x4, CH, masked(halo[...], tm * CH + CH))
            put(x5, 0, conv(x4, 0, 3, ROWS4))
    for by in (1, 3, 2):
        share2(by)
    for k in range(3, PLAIN):
        flows["p", k].wait_recv()
    put(x6, 0, conv(x5, 3, 3, 128))
    pos_forward(1)
    for by in (0, 1, 3, 2):
        flows["q", by].wait_recv()
    put(x7, 0, conv(x6, 6, 2, 64))
    last = conv(x7, 8, 2, 32)
    normed = norm(last) * gain_ref[...] + nbias_ref[...]
    nbuf[0] = normed.astype(jnp.bfloat16)

    act_flows = {}

    for j in (1, 3, 2):
        act_flows["z", j] = send(
            nbuf.at[0], nbuf.at[j], a_send.at[j - 1], a_recv.at[j - 1], at_zh(j)
        )
    for by in (1, 3, 2):
        flows["w", by].wait_recv()
        flows["c", by].wait_recv()
    row = lax.broadcasted_iota(jnp.int32, (32, GW), 0)

    def project(first, count):
        rows = nbuf[pl.ds(first, count)].reshape(count * 32, CH)
        mine = [None] * 4
        for group in range(4):
            hidden = lax.dot_general(
                rows, pwbuf[group], (((1,), (1,)), ((), ())),
                preferred_element_type=jnp.float32,
            )
            hidden = hidden + bbuf[group, pl.ds(0, 1), pl.ds(0, GW)].astype(jnp.float32)
            for j in range(first, first + count):
                source = lax.rem(zh - j + 4, 4) * 4 + y
                part = hidden[(j - first) * 32 : (j - first) * 32 + 32]
                part = jnp.where((source * 32 + row) * 320 < length, part, 0.0)
                part = jnp.concatenate([part, jnp.zeros((32, 128 - GW), jnp.float32)], axis=1)
                part = part.astype(jnp.bfloat16)
                sbuf[j, group] = part
                mine[j] = part if group == 0 else jnp.where(group == y, part, mine[j])
        for j in range(first, first + count):
            source = lax.rem(zh - j + 4, 4) * 4 + y
            for by in (1, 3, 2):
                j_send = len(act_flows)
                act_flows["y", j, by] = send(
                    sbuf.at[j, lax.rem(y + by, 4)], hbuf.at[source],
                    a_send.at[j_send], a_recv.at[j_send], at_y(by),
                )
            hbuf[source] = mine[j]

    project(0, 1)
    pos_forward(2)
    pos_forward(3)
    pos_relay(0)
    pos_relay(1)
    pos_relay(2)
    pos_relay(3)
    for j in (1, 3, 2):
        act_flows["z", j].wait_recv()
    project(1, 3)
    pos_swap(0)
    pos_swap(1)
    for j in range(4):
        for by in (1, 2, 3):
            act_flows["y", j, by].wait_recv()
    hf[pl.ds(64, CH), :] = hbuf[...].reshape(CH, 128).astype(jnp.float32)
    for tap in range(16):
        x16[:, pl.ds(tap * 128, 128)] = hf[pl.ds(tap, 624), :].astype(jnp.bfloat16)
    pos_swap(2)
    pos_swap(3)
    for j in range(4):
        for dx in (0, 1, -1, 2):
            pos_flows["p", j, dx].wait_recv()
    total = None
    for m in range(4):
        weight = jnp.concatenate(
            [pbuf[m // 2, m % 2, q].reshape(256, 512) for q in range(4)], axis=1
        )
        part = lax.dot_general(
            x16[pl.ds(16 * m, 576), :], weight, (((1,), (1,)), ((), ())),
            preferred_element_type=jnp.float32,
        )
        total = part if total is None else total + part
    conv_out = total[:CH, :128] + total[64:, 128:]
    position = gelu(conv_out[:, :GW] + posb_ref[...])
    encoded = hf[pl.ds(64, CH), pl.ds(0, GW)] + position
    out_ref[...] = encoded.T.astype(jnp.bfloat16)
    for copy in started:
        copy.wait_send()


def local(
    frames, lengths, fourth_conv, fifth_conv, sixth_conv, seventh_conv,
    norm_gain, norm_bias, project_weight, project_bias, position_weight, position_bias,
):
    vmem = pl.BlockSpec(memory_space=pltpu.VMEM)
    hbm = pl.BlockSpec(memory_space=pl.ANY)
    smem = pl.BlockSpec(memory_space=pltpu.SMEM)
    dma = pltpu.SemaphoreType.DMA
    out = pl.pallas_call(
        kernel,
        out_shape=jax.ShapeDtypeStruct((GW, CH), jnp.bfloat16),
        in_specs=[smem, hbm, hbm, hbm, hbm, hbm, vmem, vmem, hbm, vmem, hbm, vmem],
        out_specs=vmem,
        scratch_shapes=[
            pltpu.VMEM((N_TAPS, 4, 2, 4, 16, CH), jnp.bfloat16),
            pltpu.VMEM((4, 16, CH), jnp.bfloat16),
            pltpu.VMEM((2, 2, 4, 2, 128, 512), jnp.bfloat16),
            pltpu.VMEM((CH, CH), jnp.bfloat16),
            pltpu.VMEM((4, GW * GW), jnp.bfloat16),
            pltpu.VMEM((4, GW, CH), jnp.bfloat16),
            pltpu.VMEM((4, 16, 128), jnp.bfloat16),
            pltpu.VMEM((HALO, CH), jnp.bfloat16),
            pltpu.VMEM((4, CH + HALO + 32, 128), jnp.float32),
            pltpu.VMEM((4, ROWS4, 128), jnp.float32),
            pltpu.VMEM((4, 128, 128), jnp.float32),
            pltpu.VMEM((4, 64, 128), jnp.float32),
            pltpu.VMEM((4, 32, CH), jnp.bfloat16),
            pltpu.VMEM((4, 4, 32, 128), jnp.bfloat16),
            pltpu.VMEM((16, 32, 128), jnp.bfloat16),
            pltpu.VMEM((640, 128), jnp.float32),
            pltpu.VMEM((624, 2048), jnp.bfloat16),
            pltpu.VMEM((512, 128), jnp.float32),
            dma((8,)),
            dma((79,)),
            dma((79,)),
            dma((31,)),
            dma((31,)),
            dma((15,)),
            dma((15,)),
            dma,
            dma,
            pltpu.SemaphoreType.REGULAR((3,)),
        ],
        compiler_params=pltpu.CompilerParams(
            collective_id=0, has_side_effects=True, vmem_limit_bytes=60 * 1024 * 1024
        ),
    )(
        lengths, frames[0], fourth_conv, fifth_conv, sixth_conv, seventh_conv,
        norm_gain.reshape(1, CH), norm_bias.reshape(1, CH),
        project_weight.T, project_bias, position_weight[0], position_bias.reshape(1, GW),
    )
    return out[None]


def solution(mesh):
    in_specs = (
        P(("section", "dp"), "tm", None),
        P(("section", "dp")),
        P(None, ("section", "dp"), None),
        P(None, ("section", "dp"), None),
        P(None, ("section", "dp"), None),
        P(None, ("section", "dp"), None),
        P(),
        P(),
        P(None, "tm"),
        P(None, "tm"),
        P("tm", ("section", "dp"), None),
        P("tm"),
    )
    out_specs = P(("section", "dp"), "tm", None)
    return jax.shard_map(local, mesh=mesh, in_specs=in_specs, out_specs=out_specs, check_vma=False)
```

```python
import jax
import jax.numpy as jnp
from jax import lax
from jax.experimental import pallas as pl
from jax.experimental.pallas import tpu as pltpu
from jax.sharding import PartitionSpec as P

MESH = pl.DeviceIdType.MESH
CH = 512
GW = 120
EPS = 1e-05
HALO = 16
ROWS4 = 272
N_TAPS = 10
PLAIN = 6


def norm(values):
    average = jnp.mean(values, axis=-1, keepdims=True)
    centred = values - average
    spread = jnp.mean(centred * centred, axis=-1, keepdims=True)
    return centred * lax.rsqrt(spread + EPS)


def gelu(values):
    return 0.5 * values * (1.0 + lax.erf(values * 0.7071067811865476))


def kernel(
    len_ref, frames_ref, w4_ref, w5_ref, w6_ref, w7_ref, gain_ref, nbias_ref,
    pw_ref, pb_ref, pos_ref, posb_ref, out_ref,
    wbuf, stage, pbuf, fbuf, qbuf, pwbuf, bbuf, halo, x4, x5, x6, x7, nbuf, sbuf, hbuf, hf, x16, relay32,
    local_sem, w_send, w_recv, p_send, p_recv, a_send, a_recv, h_send, h_recv, rounds,
):
    section = lax.axis_index("section")
    tm = lax.axis_index("tm")
    zl = lax.axis_index("dp")
    xi = section // 2
    core = lax.rem(section, 2)
    zh = tm // 4
    y = lax.rem(tm, 4)
    direction = 1 - 2 * core

    def at_x(by):
        return (lax.rem(xi + by + 4, 4) * 2 + core, tm, zl)

    def at_z(by):
        z = lax.rem(zh * 4 + zl + by + 16, 16)
        return (section, (z // 4) * 4 + y, lax.rem(z, 4))

    def at_line(by):
        return (section, tm, lax.rem(zl + by, 4))

    def at_zh(by):
        return (section, lax.rem(zh + by, 4) * 4 + y, zl)

    def at_y(by):
        return (section, zh * 4 + lax.rem(y + by + 4, 4), zl)

    partner = (xi * 2 + 1 - core, tm, zl)
    before = (section, lax.rem(tm + 15, 16), zl)

    def signal(sem, others):
        for other in others:
            pl.semaphore_signal(sem, inc=1, device_id=other, device_id_type=MESH)

    def at_plane(dx, dz):
        by = dz * direction if dz == 2 else dz
        z = lax.rem(zh * 4 + zl + by + 16, 16)
        return (lax.rem(xi + dx + 4, 4) * 2 + core, (z // 4) * 4 + y, lax.rem(z, 4))

    barrier = pltpu.get_barrier_semaphore()
    beside = [at_x(1), at_x(-1), at_z(1), at_z(-1), at_y(1), at_y(-1)]
    signal(barrier, beside + [partner])

    fetches = []

    def fetch(src, dst):
        copy = pltpu.make_async_copy(src, dst, local_sem.at[len(fetches)])
        copy.start()
        fetches.append(copy)

    fetch(w4_ref, wbuf.at[pl.ds(0, 3), xi, core, zl])
    fetch(w5_ref, wbuf.at[pl.ds(3, 3), xi, core, zl])
    fetch(w6_ref, stage.at[pl.ds(0, 2)])
    fetch(w7_ref, stage.at[pl.ds(2, 2)])
    fetch(frames_ref, fbuf)
    fetch(pos_ref, qbuf)
    fetch(pw_ref, pwbuf.at[y])

    started = []

    def send(src, dst, send_sem, recv_sem, device):
        copy = pltpu.make_async_remote_copy(
            src_ref=src, dst_ref=dst, send_sem=send_sem, recv_sem=recv_sem,
            device_id=device, device_id_type=MESH,
        )
        copy.start()
        started.append(copy)
        return copy

    flows = {}

    def flow(name, block, device):
        j = len(flows)
        flows[name] = send(block, block, w_send.at[j], w_recv.at[j], device)

    def own(k):
        return wbuf.at[k, xi, core, zl]

    def stage0(k, by):
        device = at_plane(0, by) if k % 2 == 0 else at_plane(by, 0)
        flow(("a", k, by), own(k), device)

    def line(k, by):
        if k % 2 == 0:
            return wbuf.at[k, lax.rem(xi + by + 4, 4), core]
        return wbuf.at[k, :, core, lax.rem(zl + by + 4, 4)]

    def second(k, by):
        return at_x(by) if k % 2 == 0 else at_z(by)

    def stage1(k):
        for by in (1, -1, 2):
            flows["a", k, by].wait_recv()
        flow(("b", k, 1), line(k, 0), second(k, 1))
        flow(("b", k, -1), line(k, 0), second(k, -1))

    def pass_on(k):
        flows["b", k, 1].wait_recv()
        flows["b", k, -1].wait_recv()
        flow(("b", k, 2), line(k, -direction), second(k, direction))

    def stage2(k):
        flows["b", k, 2].wait_recv()
        flow(("p", k), wbuf.at[k, :, core], partner)

    shared = PLAIN + y

    def share0(dx, dz):
        j = len(flows)
        flows["s", dx, dz] = send(
            stage.at[y], wbuf.at[shared, xi, core, zl], w_send.at[j], w_recv.at[j],
            at_plane(dx, dz),
        )

    def lend(by):
        flow(("w", by), pwbuf.at[y], at_y(by))
        flow(("c", by), bbuf.at[y], at_y(by))

    def share1(dx):
        for dz in (0, 1, -1, 2):
            if (dx, dz) != (0, 0):
                flows["s", dx, dz].wait_recv()
        block = wbuf.at[shared, lax.rem(xi - dx + 4, 4), core]
        for by in (1, 3, 2):
            flow(("y", dx, by), block, at_y(by))

    def share2(by):
        for dx in (0, 1, -1, 2):
            flows["y", dx, by].wait_recv()
        flow(("q", by), wbuf.at[PLAIN + lax.rem(y - by + 4, 4), :, core], partner)

    pos_flows = {}

    def pos_block(x, z):
        return pbuf.at[lax.rem(x, 2), core, z, x // 2, pl.ds(0, GW)]

    def pos_send(name, block, device):
        j = len(pos_flows)
        pos_flows[name] = send(block, block, p_send.at[j], p_recv.at[j], device)

    def arrange_pos():
        values = qbuf[...].astype(jnp.float32)
        values = jnp.concatenate([values, jnp.zeros((4, 64), jnp.float32)], axis=1)
        for o in range(GW):
            relay32[pl.ds(o, 4, stride=128), :] = values[:, o * GW : o * GW + 128]
        for tap in range(4):
            pbuf[lax.rem(xi, 2), core, zl, xi // 2, :, pl.ds(tap * 128, 128)] = (
                relay32[pl.ds(tap * 128, 128), :].astype(jnp.bfloat16)
            )

    def pos_start():
        for j in (1, 2, 3):
            pos_send(("z", j), pos_block(xi, zl), at_line(j))
        pos_send(("x", 0, 1), pos_block(xi, zl), at_x(1))
        pos_send(("x", 0, -1), pos_block(xi, zl), at_x(-1))

    def pos_forward(j):
        pos_flows["z", j].wait_recv()
        block = pos_block(xi, lax.rem(zl - j + 4, 4))
        pos_send(("x", j, 1), block, at_x(1))
        pos_send(("x", j, -1), block, at_x(-1))

    def pos_relay(j):
        pos_flows["x", j, 1].wait_recv()
        pos_flows["x", j, -1].wait_recv()
        block = pos_block(lax.rem(xi - direction + 4, 4), lax.rem(zl - j + 4, 4))
        pos_send(("r", j), block, at_x(direction))
        pos_share(j)

    def pos_share(j):
        for dx in (0, 1, -1):
            block = pos_block(lax.rem(xi + dx + 4, 4), lax.rem(zl - j + 4, 4))
            pos_send(("p", j, dx), block, partner)

    def pos_swap(j):
        pos_flows["r", j].wait_recv()
        block = pos_block(lax.rem(xi + 2, 4), lax.rem(zl - j + 4, 4))
        pos_send(("p", j, 2), block, partner)

    length = len_ref[0]

    def masked(block, base):
        rows = block.shape[0]
        index = base + lax.broadcasted_iota(jnp.int32, (rows, CH), 0)
        return jnp.where(index * 20 < length, block.astype(jnp.float32), 0.0)

    def put(x_ref, start, value):
        for b in range(4):
            x_ref[b, pl.ds(start, value.shape[0]), :] = value[:, b * 128 : b * 128 + 128]

    def conv(x_ref, k, taps, rows):
        total = None
        for tap in range(taps):
            picked = jnp.concatenate(
                [x_ref[b, pl.ds(tap, rows, stride=2), :] for b in range(4)], axis=1
            ).astype(jnp.bfloat16)
            weight = wbuf[k + tap].reshape(CH, CH)
            part = jnp.dot(picked, weight, preferred_element_type=jnp.float32)
            total = part if total is None else total + part
        return gelu(norm(total)).astype(jnp.bfloat16).astype(jnp.float32)

    bias = jnp.concatenate(
        [pb_ref[...].astype(jnp.float32), jnp.zeros((1, 128 - GW), jnp.float32)], axis=1
    )
    bbuf[y] = jnp.broadcast_to(bias, (16, 128)).astype(jnp.bfloat16)
    hf[...] = jnp.zeros(hf.shape, jnp.float32)
    put(x4, CH + HALO, jnp.zeros((32, CH), jnp.float32))
    for j in range(4):
        fetches[j].wait()
    fetch(stage.at[y], wbuf.at[PLAIN + y, xi, core, zl])
    pl.semaphore_wait(barrier, 7)
    signal(rounds.at[0], beside)

    share0(0, 1)
    share0(0, -1)
    for k in range(PLAIN):
        stage0(k, 1)
        stage0(k, -1)
    share0(1, 0)
    share0(-1, 0)
    pl.semaphore_wait(rounds.at[0], 6)
    signal(rounds.at[1], [at_z(2), at_z(-2), at_x(2)])
    share0(0, 2)
    for k in range(PLAIN):
        stage0(k, 2)
    for dx, dz in ((2, 0), (1, 1), (1, -1), (-1, 1), (-1, -1)):
        share0(dx, dz)
    fetches[4].wait()
    put(x4, 0, masked(fbuf[...], tm * CH))
    pl.semaphore_wait(rounds.at[1], 3)
    signal(rounds.at[2], [at_z(4), at_z(-4)])
    for dx, dz in ((1, 2), (-1, 2), (2, 1), (2, -1), (2, 2)):
        share0(dx, dz)
    fetches[7].wait()
    share1(0)
    fetches[5].wait()
    arrange_pos()
    for k in range(PLAIN):
        stage1(k)
    pl.semaphore_wait(rounds.at[2], 2)
    halo_copy = send(frames_ref.at[pl.ds(0, HALO)], halo, h_send, h_recv, before)
    pos_start()
    share1(1)
    share1(-1)
    pass_on(0)
    pass_on(1)
    share1(2)
    fetches[6].wait()
    for by in (1, 3, 2):
        lend(by)
    for k in range(2, PLAIN):
        pass_on(k)
    flow(("q", 0), wbuf.at[shared, :, core], partner)
    for k in range(PLAIN):
        stage2(k)
        if k == 4:
            for j in range(3):
                flows["p", j].wait_recv()
            halo_copy.wait_recv()
            put(x4, CH, masked(halo[...], tm * CH + CH))
            put(x5, 0, conv(x4, 0, 3, ROWS4))
    for by in (1, 3, 2):
        share2(by)
    for k in range(3, PLAIN):
        flows["p", k].wait_recv()
    put(x6, 0, conv(x5, 3, 3, 128))
    pos_forward(1)
    for by in (0, 1, 3, 2):
        flows["q", by].wait_recv()
    put(x7, 0, conv(x6, 6, 2, 64))
    last = conv(x7, 8, 2, 32)
    normed = norm(last) * gain_ref[...] + nbias_ref[...]
    nbuf[0] = normed.astype(jnp.bfloat16)

    act_flows = {}

    for j in (1, 3, 2):
        act_flows["z", j] = send(
            nbuf.at[0], nbuf.at[j], a_send.at[j - 1], a_recv.at[j - 1], at_zh(j)
        )
    for by in (1, 3, 2):
        flows["w", by].wait_recv()
        flows["c", by].wait_recv()
    row = lax.broadcasted_iota(jnp.int32, (32, GW), 0)

    def project(first, count):
        rows = nbuf[pl.ds(first, count)].reshape(count * 32, CH)
        mine = [None] * 4
        for group in range(4):
            hidden = lax.dot_general(
                rows, pwbuf[group], (((1,), (1,)), ((), ())),
                preferred_element_type=jnp.float32,
            )
            hidden = hidden + bbuf[group, pl.ds(0, 1), pl.ds(0, GW)].astype(jnp.float32)
            for j in range(first, first + count):
                source = lax.rem(zh - j + 4, 4) * 4 + y
                part = hidden[(j - first) * 32 : (j - first) * 32 + 32]
                part = jnp.where((source * 32 + row) * 320 < length, part, 0.0)
                part = jnp.concatenate([part, jnp.zeros((32, 128 - GW), jnp.float32)], axis=1)
                part = part.astype(jnp.bfloat16)
                sbuf[j, group] = part
                mine[j] = part if group == 0 else jnp.where(group == y, part, mine[j])
        for j in range(first, first + count):
            source = lax.rem(zh - j + 4, 4) * 4 + y
            for by in (1, 3, 2):
                j_send = len(act_flows)
                act_flows["y", j, by] = send(
                    sbuf.at[j, lax.rem(y + by, 4)], hbuf.at[source],
                    a_send.at[j_send], a_recv.at[j_send], at_y(by),
                )
            hbuf[source] = mine[j]

    project(0, 1)
    pos_forward(2)
    pos_forward(3)
    pos_relay(0)
    pos_relay(1)
    pos_relay(2)
    pos_relay(3)
    for j in (1, 3, 2):
        act_flows["z", j].wait_recv()
    project(1, 3)
    pos_swap(0)
    pos_swap(1)
    for j in range(4):
        for by in (1, 2, 3):
            act_flows["y", j, by].wait_recv()
    hf[pl.ds(64, CH), :] = hbuf[...].reshape(CH, 128).astype(jnp.float32)
    for tap in range(16):
        x16[:, pl.ds(tap * 128, 128)] = hf[pl.ds(tap, 624), :].astype(jnp.bfloat16)
    pos_swap(2)
    pos_swap(3)
    for j in range(4):
        for dx in (0, 1, -1, 2):
            pos_flows["p", j, dx].wait_recv()
    total = None
    for m in range(4):
        weight = jnp.concatenate(
            [pbuf[m // 2, m % 2, q].reshape(256, 512) for q in range(4)], axis=1
        )
        part = lax.dot_general(
            x16[pl.ds(16 * m, 576), :], weight, (((1,), (1,)), ((), ())),
            preferred_element_type=jnp.float32,
        )
        total = part if total is None else total + part
    conv_out = total[:CH, :128] + total[64:, 128:]
    position = gelu(conv_out[:, :GW] + posb_ref[...])
    encoded = hf[pl.ds(64, CH), pl.ds(0, GW)] + position
    out_ref[...] = encoded.T.astype(jnp.bfloat16)
    for copy in started:
        copy.wait_send()


def local(
    frames, lengths, fourth_conv, fifth_conv, sixth_conv, seventh_conv,
    norm_gain, norm_bias, project_weight, project_bias, position_weight, position_bias,
):
    vmem = pl.BlockSpec(memory_space=pltpu.VMEM)
    hbm = pl.BlockSpec(memory_space=pl.ANY)
    smem = pl.BlockSpec(memory_space=pltpu.SMEM)
    dma = pltpu.SemaphoreType.DMA
    out = pl.pallas_call(
        kernel,
        out_shape=jax.ShapeDtypeStruct((GW, CH), jnp.bfloat16),
        in_specs=[smem, hbm, hbm, hbm, hbm, hbm, vmem, vmem, hbm, vmem, hbm, vmem],
        out_specs=vmem,
        scratch_shapes=[
            pltpu.VMEM((N_TAPS, 4, 2, 4, 16, CH), jnp.bfloat16),
            pltpu.VMEM((4, 16, CH), jnp.bfloat16),
            pltpu.VMEM((2, 2, 4, 2, 128, 512), jnp.bfloat16),
            pltpu.VMEM((CH, CH), jnp.bfloat16),
            pltpu.VMEM((4, GW * GW), jnp.bfloat16),
            pltpu.VMEM((4, GW, CH), jnp.bfloat16),
            pltpu.VMEM((4, 16, 128), jnp.bfloat16),
            pltpu.VMEM((HALO, CH), jnp.bfloat16),
            pltpu.VMEM((4, CH + HALO + 32, 128), jnp.float32),
            pltpu.VMEM((4, ROWS4, 128), jnp.float32),
            pltpu.VMEM((4, 128, 128), jnp.float32),
            pltpu.VMEM((4, 64, 128), jnp.float32),
            pltpu.VMEM((4, 32, CH), jnp.bfloat16),
            pltpu.VMEM((4, 4, 32, 128), jnp.bfloat16),
            pltpu.VMEM((16, 32, 128), jnp.bfloat16),
            pltpu.VMEM((640, 128), jnp.float32),
            pltpu.VMEM((624, 2048), jnp.bfloat16),
            pltpu.VMEM((512, 128), jnp.float32),
            dma((8,)),
            dma((79,)),
            dma((79,)),
            dma((31,)),
            dma((31,)),
            dma((15,)),
            dma((15,)),
            dma,
            dma,
            pltpu.SemaphoreType.REGULAR((3,)),
        ],
        compiler_params=pltpu.CompilerParams(
            collective_id=0, has_side_effects=True, vmem_limit_bytes=60 * 1024 * 1024
        ),
    )(
        lengths, frames[0], fourth_conv, fifth_conv, sixth_conv, seventh_conv,
        norm_gain.reshape(1, CH), norm_bias.reshape(1, CH),
        project_weight.T, project_bias, position_weight[0], position_bias.reshape(1, GW),
    )
    return out[None]


def solution(mesh):
    in_specs = (
        P(("section", "dp"), "tm", None),
        P(("section", "dp")),
        P(None, ("section", "dp"), None),
        P(None, ("section", "dp"), None),
        P(None, ("section", "dp"), None),
        P(None, ("section", "dp"), None),
        P(),
        P(),
        P(None, "tm"),
        P(None, "tm"),
        P("tm", ("section", "dp"), None),
        P("tm"),
    )
    out_specs = P(("section", "dp"), "tm", None)
    return jax.shard_map(local, mesh=mesh, in_specs=in_specs, out_specs=out_specs, check_vma=False)
```
